256 devices in a mesh: facet: 16 (over y, x_hi, core), bl: 16 (over z, x_lo).
Axes of the slice: x: 4 (x_hi: 2, x_lo: 2; x = x_hi * 2 + x_lo), y: 4, z: 8, core: 2. Of those that a mesh axis runs over, the one named last changes fastest.
Arguments:
- facet_model: bfloat16 [16, 1024, 1024], P('facet', 'bl'), may hold values from -0.005859375 to 0.005859375
- screens: bfloat16 [16, 256, 64, 128], P('facet', 'bl'), may hold values from 0.099609375 to 1.8984375
- observed: float32 [192, 64, 128], P('bl'), may hold values from -24 to 24
- offsets: int32 [192, 2], P('bl'), may hold values from 0 to 4032
- stations: int32 [192, 2], P('bl'), may hold values from 0 to 255
- counts: int32 [16], P('bl'), may hold values from 1 to 12, as said below
Outputs:
- residual_vis: float32 [192, 64, 128], P('bl')
- residual_image: float32 [16, 1024, 1024], P('facet', 'bl')
The draws below stay inside these ranges and needn't reach their ends.
Inputs may be any that keep to these rules, and one draw needn't show every extreme that they name: `counts`: some baseline block has all 12 slots live.
All inputs are finite; a program needn't handle non-finite values.
Results may differ from the reference program's by a relative error of at most 0.0061.
Values may be sent and summed in bfloat16 or wider, within the bound.
No kernel may reach another device: no remote copies, remote signals or barrier semaphores. Data moves between devices by JAX's collectives and lax.ppermute only.
A program may use at most 64 MiB of HBM per device.

```python
import math
import jax
import jax.numpy as jnp
from jax import lax

FACET_PX = 1024
G = 64
STATIONS = 256
FGRID = 4
T_DEV = 12
NF = 16
NBLK = 16
TILES = 192
NIMG = 4096


def draw_counts(key, part):
    first_key, second_key = jax.random.split(jax.random.fold_in(key, 11))
    values = jax.random.randint(first_key, (NBLK,), 1, T_DEV + 1)
    fullest = jax.random.randint(second_key, (), 0, NBLK)
    return jnp.where(jnp.arange(NBLK) == fullest, T_DEV, values).astype(jnp.int32)


def with_ends(array, rng, low, largest):
    longest = array.shape.index(max(array.shape))
    spots = []
    for shift in (0, 1):
        where = [jax.random.randint(jax.random.fold_in(rng, axis), (), 0, length) for axis, length in enumerate(array.shape)]
        where[longest] = (where[longest] + shift) % array.shape[longest]
        spots.append(tuple(where))
    return array.at[spots[0]].set(low).at[spots[1]].set(largest)


def levels(stream_key, shape, cuts, low, high):
    level = 1.0
    for axis_at, blocks in cuts:
        draws = jax.random.uniform(jax.random.fold_in(jax.random.fold_in(stream_key, 6), axis_at), (blocks,), jnp.float32, low / len(cuts), high / len(cuts))
        level = level * jnp.repeat(jnp.exp(draws), shape[axis_at] // blocks).reshape((-1,) + (1,) * (len(shape) - 1 - axis_at))
    return level


def gaussian(key, shape, spread, reach, cuts=(), kind=jnp.bfloat16):
    drawn = jax.random.normal(key, shape, jnp.float32) * spread
    if len(cuts) > 0:
        drawn = levels(key, shape, cuts, -0.22, 0.18) * drawn
    return jnp.clip(drawn, min=-reach, max=reach).astype(kind)


def setup_inputs(seed: int = 0) -> dict:
    arg_keys = jax.random.split(jax.random.key(seed), 7)
    facet_model = gaussian(arg_keys[0], (NF, FACET_PX, FACET_PX), (1.0 / FACET_PX), 0.005859375, ((0, 16), (1, 16)))
    screens = jnp.clip(1.0 + 0.18 * jax.random.normal(arg_keys[1], (NF, STATIONS, G, 2 * G), jnp.float32), 0.099609375, 1.8984375).astype(jnp.bfloat16)
    observed = gaussian(arg_keys[2], (TILES, G, 2 * G), 4.0, 24.0, ((0, 16),), jnp.float32)
    offsets = with_ends(jax.random.randint(arg_keys[3], (TILES, 2), 0, NIMG - G + 1), jax.random.fold_in(arg_keys[3], 1), 0, NIMG - G).astype(jnp.int32)
    stations = with_ends(jax.random.randint(arg_keys[4], (TILES, 2), 0, STATIONS), jax.random.fold_in(arg_keys[4], 1), 0, STATIONS - 1).astype(jnp.int32)
    counts = draw_counts(jax.random.fold_in(arg_keys[6], 71), 0)
    return {"facet_model": facet_model, "screens": screens, "observed": observed, "offsets": offsets, "stations": stations, "counts": counts}


def tables(offset_u, offset_v, facet_id, tile_width, facet_cells):
    grid_cells = FGRID * facet_cells
    corner_x = facet_id // FGRID * facet_cells
    corner_y = facet_id % FGRID * facet_cells
    pixel_index = jnp.arange(facet_cells, dtype=jnp.int32)
    cell_index = jnp.arange(tile_width, dtype=jnp.int32)
    phase_u = jnp.mod((offset_u + cell_index)[:, None] * (corner_x + pixel_index)[None, :], grid_cells)
    phase_v = jnp.mod((offset_v + cell_index)[:, None] * (corner_y + pixel_index)[None, :], grid_cells)
    angle_u = phase_u.astype(jnp.float32) * (2.0 * math.pi / grid_cells)
    angle_v = phase_v.astype(jnp.float32) * (2.0 * math.pi / grid_cells)
    tab_u = jnp.concatenate([jnp.cos(angle_u), -jnp.sin(angle_u)], axis=0).astype(jnp.bfloat16)
    table_vertical = jnp.concatenate([jnp.cos(angle_v), jnp.sin(angle_v)], axis=0).astype(jnp.bfloat16)
    return (tab_u, table_vertical)

def half_splits(value):
    half_width = value.shape[-1] // 2
    return (value[..., :half_width], value[..., half_width:])

def complex_times(left_re, left_im, right_re, right_im):
    return (left_re * right_re - left_im * right_im, left_re * right_im + left_im * right_re)

def times_conj(left_re, left_im, right_re, right_im):
    return (left_re * right_re + left_im * right_im, left_im * right_re - left_re * right_im)

def reference(facet_model, screens, observed, offsets, stations, counts):
    tile_width = observed.shape[1]
    facet_cells = facet_model.shape[1]
    tile_total = observed.shape[0]
    per_block = tile_total // counts.shape[0]
    slot_index = jnp.arange(tile_total, dtype=jnp.int32)
    live_mask = slot_index % per_block < jnp.repeat(counts, per_block)
    facet_ids = jnp.arange(NF, dtype=jnp.int32)

    def predict_tile(tile_args):
        tile_offset, tile_couple = tile_args

        def facet_step(running, facet_id):
            tab_u, table_vertical = tables(tile_offset[0], tile_offset[1], facet_id, tile_width, facet_cells)
            upper_portion = jnp.dot(tab_u, facet_model[facet_id], preferred_element_type=jnp.float32).astype(jnp.bfloat16)
            block_groups = jnp.dot(upper_portion, table_vertical.T, preferred_element_type=jnp.float32)
            real_part = block_groups[:tile_width, :tile_width] + block_groups[tile_width:, tile_width:]
            imag_part = block_groups[tile_width:, :tile_width] - block_groups[:tile_width, tile_width:]
            first_station_gain = screens[facet_id, tile_couple[0]].astype(jnp.float32)
            gain_q = screens[facet_id, tile_couple[1]].astype(jnp.float32)
            p_re, p_im = half_splits(first_station_gain)
            q_re, q_im = half_splits(gain_q)
            y_re, y_im = complex_times(p_re, p_im, real_part, imag_part)
            x_re, x_im = times_conj(y_re, y_im, q_re, q_im)
            return (running + jnp.concatenate([x_re, x_im], axis=1), None)
        running, _ = lax.scan(facet_step, jnp.zeros((tile_width, 2 * tile_width), jnp.float32), facet_ids)
        return running
    predicted = lax.map(predict_tile, (offsets, stations))
    residual_vis = jnp.where(live_mask[:, None, None], observed - predicted, jnp.zeros_like(observed))
    image_scale = 1.0 / (32.0 * tile_width * math.sqrt(tile_total))

    def image_facet(facet_id):

        def tile_step(running, tile_args):
            tile_offset, tile_couple, tile_resid = tile_args
            tab_u, table_vertical = tables(tile_offset[0], tile_offset[1], facet_id, tile_width, facet_cells)
            first_station_gain = screens[facet_id, tile_couple[0]].astype(jnp.float32)
            gain_q = screens[facet_id, tile_couple[1]].astype(jnp.float32)
            p_re, p_im = half_splits(first_station_gain)
            q_re, q_im = half_splits(gain_q)
            r_re, r_im = half_splits(tile_resid)
            z_re, z_im = times_conj(r_re, r_im, p_re, p_im)
            w_re, w_im = complex_times(z_re, z_im, q_re, q_im)
            w_re = w_re.astype(jnp.bfloat16)
            w_im = w_im.astype(jnp.bfloat16)
            stacked = jnp.concatenate([jnp.concatenate([w_re, -w_im], axis=1), jnp.concatenate([w_im, w_re], axis=1)], axis=0)
            q_two = jnp.dot(stacked, table_vertical, preferred_element_type=jnp.float32).astype(jnp.bfloat16)
            return (running + jnp.dot(tab_u.T, q_two, preferred_element_type=jnp.float32), None)
        running, _ = lax.scan(tile_step, jnp.zeros((facet_cells, facet_cells), jnp.float32), (offsets, stations, residual_vis))
        return running * image_scale
    residual_image = lax.map(image_facet, facet_ids)
    return (residual_vis, residual_image)
```

```python
import math

import jax
import jax.numpy as jnp
from jax import lax
from jax.experimental import pallas as pl
from jax.experimental.pallas import tpu as pltpu
from jax.sharding import PartitionSpec as P

FGRID = 4
NX = 2


def wave(count, start, length, cells, dtype=jnp.float32):
    pixel = start + jnp.arange(length, dtype=jnp.int32)
    turn = jnp.mod(count[:, None] * pixel[None, :], cells)
    angle = turn.astype(jnp.float32) * (2.0 * math.pi / cells)
    return jnp.cos(angle), jnp.sin(angle)


def take_kernel(block_ref, row_ref, *refs):
    *blocks, out_ref, sems = refs
    slots = out_ref.shape[0]

    def begin(slot, carry):
        which = block_ref[slot]
        row = row_ref[slot]
        for number, block in enumerate(blocks):

            @pl.when(which == number)
            def _():
                pltpu.make_async_copy(block.at[row], out_ref.at[slot], sems.at[slot]).start()

        return carry

    def finish(slot, carry):
        pltpu.make_async_copy(blocks[0].at[0], out_ref.at[slot], sems.at[slot]).wait()
        return carry

    lax.fori_loop(0, slots, begin, 0)
    lax.fori_loop(0, slots, finish, 0)


def take(blocks, which, row):
    slots = which.shape[0]
    shape = (slots,) + blocks[0].shape[1:]
    return pl.pallas_call(
        take_kernel,
        out_shape=jax.ShapeDtypeStruct(shape, blocks[0].dtype),
        in_specs=[pl.BlockSpec(memory_space=pltpu.SMEM)] * 2
        + [pl.BlockSpec(memory_space=pl.ANY)] * len(blocks),
        out_specs=pl.BlockSpec(memory_space=pltpu.VMEM),
        scratch_shapes=[pltpu.SemaphoreType.DMA((slots,))],
        name="take_screens",
    )(which, row, *blocks)


def per_device(facet_model, screens, observed, offsets, stations, counts):
    tiles, width, wide = observed.shape
    cells = facet_model.shape[2]
    rows = facet_model.shape[1]
    bl = lax.axis_size("bl")
    nz = bl // NX
    nf = lax.axis_size("facet")
    grid = FGRID * cells
    facet = lax.axis_index("facet")
    here = lax.axis_index("bl")
    z, xl = here // NX, here % NX
    fx = facet // FGRID * cells
    fy = facet % FGRID * cells
    own = screens.shape[1]

    def zshift(value, by):
        pairs = [(a * NX + b, (a + by) % nz * NX + b) for a in range(nz) for b in range(NX)]
        return lax.ppermute(value, "bl", pairs)

    def swap(value):
        return lax.ppermute(value, "bl", [(i, i ^ 1) for i in range(bl)])

    def gather_z(block):
        half = block.shape[0] // 2
        up, down = [block], [block]
        for _ in range(nz // 2 - 1):
            up.append(zshift(up[-1], 1))
            down.append(zshift(down[-1], -1))
        first = zshift(up[-1][:half], 1)
        second = zshift(down[-1][half:], -1)
        return up[1:], down[1:], first, second

    both = jnp.concatenate([offsets, stations], axis=0)
    both = jnp.concatenate([both, swap(both)], axis=1)
    offs = jnp.concatenate([both[:tiles, :2], both[:tiles, 2:]], axis=0)
    stas = jnp.concatenate([both[tiles:, :2], both[tiles:, 2:]], axis=0)

    m_up, m_down, m_first, m_second = gather_z(facet_model[0])
    s_up, s_down, s_first, s_second = gather_z(screens[0])

    cell = jnp.arange(width, dtype=jnp.int32)
    ev_c, ev_s = wave(cell, fy, cells, grid)
    ov_c, ov_s = wave(offs[:, 1], fy, cells, grid)
    tv_c = ov_c[:, None] * ev_c[None] - ov_s[:, None] * ev_s[None]
    tv_s = ov_s[:, None] * ev_c[None] + ov_c[:, None] * ev_s[None]
    tab_v = jnp.concatenate([tv_c.astype(jnp.bfloat16), tv_s.astype(jnp.bfloat16)], axis=1)

    half_x = cells // NX
    place = jnp.arange(half_x, dtype=jnp.int32)
    pixel = fx + (place // rows * NX + xl) * rows + place % rows

    def wave_u(count):
        angle = jnp.mod(count[:, None] * pixel[None], grid).astype(jnp.float32)
        angle = angle * (2.0 * math.pi / grid)
        return jnp.cos(angle), jnp.sin(angle)

    eu_c, eu_s = wave_u(cell)
    ou_c, ou_s = wave_u(offs[:, 0])
    tu_c = ou_c[:, None] * eu_c[None] - ou_s[:, None] * eu_s[None]
    tu_s = ou_s[:, None] * eu_c[None] + ou_c[:, None] * eu_s[None]
    tab_u = jnp.concatenate([tu_c.astype(jnp.bfloat16), -tu_s.astype(jnp.bfloat16)], axis=1)

    model = jnp.zeros((nz, rows, cells), jnp.bfloat16)
    opposite = jnp.concatenate([m_first, m_second], axis=0)
    model = lax.dynamic_update_index_in_dim(model, facet_model[0], z, 0)
    model = lax.dynamic_update_index_in_dim(model, opposite, (z + nz // 2) % nz, 0)
    for step in range(1, nz // 2):
        model = lax.dynamic_update_index_in_dim(model, m_up[step - 1], (z - step) % nz, 0)
        model = lax.dynamic_update_index_in_dim(model, m_down[step - 1], (z + step) % nz, 0)
    upper = jnp.einsum(
        "tkn,np->tkp", tab_u, model.reshape(half_x, cells), preferred_element_type=jnp.float32
    ).astype(jnp.bfloat16)
    blocks = jnp.einsum("gsf,gmf->gsm", upper, tab_v, preferred_element_type=jnp.float32)
    part_re = blocks[:, :width, :width] + blocks[:, width:, width:]
    part_im = blocks[:, width:, :width] - blocks[:, :width, width:]
    part = jnp.concatenate([part_re, part_im], axis=2)
    other = swap(part[tiles:].astype(jnp.bfloat16)).astype(jnp.float32)
    s_re = part_re[:tiles] + other[..., :width]
    s_im = part_im[:tiles] + other[..., width:]

    wanted = jnp.concatenate([stas[:, 0], stas[:, 1]])
    owner = wanted // own
    held = owner % NX == xl
    away = (owner // NX - z) % nz
    row = wanted % own
    far = nz // 2
    lower = (away == far) & (row >= own // 2)
    gain_blocks = [screens[0]] + s_down + [s_first] + s_up[::-1] + [s_second]
    which = jnp.where(lower, nz, away)
    row = jnp.where(away == far, row % (own // 2), row)
    picked = take(gain_blocks, which, row).reshape(2, 2, tiles, width, wide)
    held = held.reshape(2, 2, tiles)[:, 0, :, None, None]
    gains = jnp.where(held, picked[:, 0], swap(picked[:, 1])).astype(jnp.float32)
    p_re, p_im = gains[0, ..., :width], gains[0, ..., width:]
    q_re, q_im = gains[1, ..., :width], gains[1, ..., width:]
    g_re = p_re * q_re + p_im * q_im
    g_im = p_im * q_re - p_re * q_im

    share = tiles * width // nf
    contribution = jnp.concatenate(
        [g_re * s_re - g_im * s_im, g_re * s_im + g_im * s_re], axis=2
    ).astype(jnp.bfloat16)
    arrived = lax.all_to_all(contribution.reshape(nf, share, wide), "facet", 0, 0)
    total = jnp.sum(arrived.astype(jnp.float32), axis=0).astype(jnp.bfloat16)
    predicted = lax.all_to_all(
        jnp.broadcast_to(total[None], (nf, share, wide)), "facet", 0, 0
    ).reshape(tiles, width, wide)
    live = (jnp.arange(tiles, dtype=jnp.int32) < counts[0])[:, None, None]
    residual = jnp.where(live, observed - predicted.astype(jnp.float32), 0.0)

    r_re, r_im = residual[..., :width], residual[..., width:]
    w_re = (g_re * r_re + g_im * r_im).astype(jnp.bfloat16)
    w_im = (g_re * r_im - g_im * r_re).astype(jnp.bfloat16)
    w = jnp.concatenate([w_re, w_im], axis=2)
    w = jnp.concatenate([w, swap(w)], axis=0)
    w_re, w_im = w[..., :width], w[..., width:]
    stacked = jnp.concatenate(
        [jnp.concatenate([w_re, -w_im], axis=2), jnp.concatenate([w_im, w_re], axis=2)], axis=1
    )
    q_two = jnp.einsum(
        "tuk,tky->tuy", stacked, tab_v, preferred_element_type=jnp.float32
    ).astype(jnp.bfloat16)
    image = jnp.einsum("tkx,tky->xy", tab_u, q_two, preferred_element_type=jnp.float32)
    image = image.astype(jnp.bfloat16).reshape(nz, rows, cells)
    groups = [[a * NX + b for a in range(nz)] for b in range(NX)]
    image = lax.all_to_all(image, "bl", 0, 0, axis_index_groups=groups)
    scale = 1.0 / (32.0 * width * math.sqrt(tiles * bl))
    residual_image = (jnp.sum(image.astype(jnp.float32), axis=0) * scale)[None]
    return (residual, residual_image)


def solution(mesh):
    in_specs = (
        P("facet", "bl", None),
        P("facet", "bl", None, None),
        P("bl", None, None),
        P("bl", None),
        P("bl", None),
        P("bl"),
    )
    out_specs = (P("bl", None, None), P("facet", "bl", None))
    return jax.shard_map(
        per_device, mesh=mesh, in_specs=in_specs, out_specs=out_specs, check_vma=False
    )
```

```python
import functools
import math

import jax
import jax.numpy as jnp
from jax import lax
from jax.experimental import pallas as pl
from jax.experimental.pallas import tpu as pltpu
from jax.sharding import PartitionSpec as P

FGRID = 4
NX = 2


def wave(count, pixel, cells):
    turn = jnp.mod(count[:, None] * pixel[None, :], cells)
    angle = turn.astype(jnp.float32) * (2.0 * math.pi / cells)
    return jnp.cos(angle), jnp.sin(angle)


def times(a, b):
    half = a.shape[-1] // 2
    turned = pltpu.roll(b, half, 1)
    same, cross = a * b, a * turned
    real = lax.broadcasted_iota(jnp.int32, a.shape, 1) < half
    return jnp.where(real, same - pltpu.roll(same, half, 1), cross + pltpu.roll(cross, half, 1))


def times_conj(a, b):
    half = a.shape[-1] // 2
    turned = pltpu.roll(b, half, 1)
    same, cross = a * b, a * turned
    real = lax.broadcasted_iota(jnp.int32, a.shape, 1) < half
    return jnp.where(real, same + pltpu.roll(same, half, 1), cross - pltpu.roll(cross, half, 1))


def split(number, by):
    if by & (by - 1) == 0:
        return lax.shift_right_logical(number, by.bit_length() - 1), number & (by - 1)
    return number // by, lax.rem(number, by)


def choose(which, low, high, act):
    if high - low == 1:
        act(low)
        return
    mid = (low + high) // 2

    @pl.when(which < mid)
    def _():
        choose(which, low, mid, act)

    @pl.when(which >= mid)
    def _():
        choose(which, mid, high, act)


def begin_take(place_ref, station_ref, blocks, picked, sems, tiles, own, nz):
    half = blocks[-1].shape[0]
    skip = blocks[0].shape[0] - own
    here = place_ref[0]
    z = split(here, NX)[0]

    def begin(slot, carry):
        side = (slot >= tiles).astype(jnp.int32)
        station = station_ref[tiles + slot - side * tiles, side]
        owner, row = split(station, own)
        away = split(split(owner, NX)[0] - z + nz, nz)[1]
        row = row + skip
        late = jnp.logical_and(away == nz // 2, row >= half)
        which = jnp.where(late, nz, away)
        row = jnp.where(late, row - half, row)

        def act(number):
            pltpu.make_async_copy(
                blocks[number].at[row], picked.at[slot], sems.at[slot]
            ).start()

        choose(which, 0, len(blocks), act)
        return carry

    lax.fori_loop(0, 2 * tiles, begin, 0)


def end_take(place_ref, station_ref, blocks, picked, sems, tiles, own, tile):
    xl = split(place_ref[0], NX)[1]
    width = picked.shape[2] // 2
    one = jnp.where(
        lax.broadcasted_iota(jnp.int32, picked.shape[1:], 1) < width, 1.0, 0.0
    ).astype(jnp.float32)
    found = []
    for side in range(2):
        slot = side * tiles + tile
        pltpu.make_async_copy(blocks[0].at[0], picked.at[slot], sems.at[slot]).wait()
        station = station_ref[tiles + tile, side]
        here = (split(split(station, own)[0], NX)[1] == xl).astype(jnp.float32)
        found.append(picked[slot].astype(jnp.float32) * here + one * (1.0 - here))
    return times_conj(*found)


def far_gain_kernel(own, nz, place_ref, station_ref, *refs):
    *blocks, x_ref, picked, sems = refs
    tiles = x_ref.shape[0]
    begin_take(place_ref, station_ref, blocks, picked, sems, tiles, own, nz)
    for tile in range(tiles):
        value = end_take(place_ref, station_ref, blocks, picked, sems, tiles, own, tile)
        x_ref[tile] = value.astype(x_ref.dtype)


def own_gain_kernel(own, nz, place_ref, station_ref, x_ref, s_ref, other_ref, *refs):
    *blocks, gain_ref, keep_ref, give_ref, picked, sems = refs
    tiles = x_ref.shape[0]
    part = tiles // 2
    core = place_ref[1]
    begin_take(place_ref, station_ref, blocks, picked, sems, tiles, own, nz)
    for tile in range(tiles):
        gain = end_take(place_ref, station_ref, blocks, picked, sems, tiles, own, tile)
        gain = times(gain, x_ref[tile].astype(jnp.float32))
        gain_ref[tile] = gain
        value = times(gain, s_ref[tile] + other_ref[tile].astype(jnp.float32))

        @pl.when(core == tile // part)
        def _():
            keep_ref[tile % part] = value

        @pl.when(core != tile // part)
        def _():
            give_ref[tile % part] = value


def gain_call(kernel, name, own, nz, place, stations, dense, blocks, outs, tiles):
    shape = blocks[0].shape[1:]
    return pl.pallas_call(
        functools.partial(kernel, own, nz),
        out_shape=[jax.ShapeDtypeStruct((count,) + shape, kind) for count, kind in outs],
        in_specs=[pl.BlockSpec(memory_space=pltpu.SMEM)] * 2
        + [pl.BlockSpec(memory_space=pltpu.VMEM)] * len(dense)
        + [pl.BlockSpec(memory_space=pl.ANY)] * len(blocks),
        out_specs=[pl.BlockSpec(memory_space=pltpu.VMEM)] * len(outs),
        scratch_shapes=[
            pltpu.VMEM((2 * tiles,) + shape, blocks[0].dtype),
            pltpu.SemaphoreType.DMA((2 * tiles,)),
        ],
        name=name,
    )(place, stations, *dense, *blocks)


def predict_kernel(u_ref, v_ref, *refs):
    *blocks, s_ref, model = refs
    rows = blocks[0].shape[1]
    wide = blocks[0].shape[2]

    @pl.when(pl.program_id(0) == 0)
    def _():
        for number, block in enumerate(blocks):
            for lane in range(model.shape[1] // wide):
                model[number * rows : (number + 1) * rows, lane * wide : (lane + 1) * wide] = block[
                    lane
                ]

    count, height, deep = u_ref.shape
    upper = jnp.dot(
        u_ref[...].reshape(count * height, deep), model[...], preferred_element_type=jnp.float32
    ).astype(jnp.bfloat16)
    half = height // 2
    for tile in range(count):
        both = lax.dot_general(
            upper[tile * height : (tile + 1) * height],
            v_ref[tile],
            (((1,), (1,)), ((), ())),
            preferred_element_type=jnp.float32,
        )
        top, low = both[:half], pltpu.roll(both[half:], half, 1)
        real = lax.broadcasted_iota(jnp.int32, top.shape, 1) < half
        s_ref[tile] = jnp.where(real, top + low, low - top).astype(s_ref.dtype)


def predict_call(name, tab_u, tab_v, blocks, kind, first, tiles, step):
    height, deep = tab_u.shape[1:]
    cells = tab_v.shape[2]
    rows, wide = blocks[0].shape[1:]
    lanes = cells // wide
    begin = first // step
    return pl.pallas_call(
        predict_kernel,
        grid=(tiles // step,),
        out_shape=jax.ShapeDtypeStruct((tiles, height // 2, height), kind),
        in_specs=[
            pl.BlockSpec((step, height, deep), lambda i: (begin + i, 0, 0)),
            pl.BlockSpec((step, height, cells), lambda i: (begin + i, 0, 0)),
        ]
        + [pl.BlockSpec((lanes, rows, wide), lambda i: (0, 0, 0))] * len(blocks),
        out_specs=pl.BlockSpec((step, height // 2, height), lambda i: (i, 0, 0)),
        scratch_shapes=[pltpu.VMEM((deep, cells), tab_u.dtype)],
        name=name,
    )(tab_u, tab_v, *blocks)


def residual_kernel(place_ref, count_ref, keep_ref, others_ref, seen_ref, gain_ref, res_ref, w_ref):
    tiles = seen_ref.shape[0]
    part = tiles // 2
    core = place_ref[1]
    count = count_ref[0]
    for tile in range(tiles):
        live = (tile < count).astype(jnp.int32)
        mine = (core == tile // part).astype(jnp.float32)
        value = keep_ref[tile % part] * mine + others_ref[tile % part] * (1.0 - mine)
        alive = lax.broadcasted_iota(jnp.int32, value.shape, 0) >= (1 - live) * value.shape[0]
        value = jnp.where(alive, seen_ref[tile] - value, 0.0)
        res_ref[tile] = value
        w_ref[tile] = times_conj(value, gain_ref[tile]).astype(w_ref.dtype)


def per_device(facet_model, screens, observed, offsets, stations, counts):
    tiles, width, wide = observed.shape
    cells = facet_model.shape[2]
    rows = facet_model.shape[1]
    bl = lax.axis_size("bl")
    nz = bl // NX
    nf = lax.axis_size("facet")
    grid = FGRID * cells
    facet = lax.axis_index("facet")
    here = lax.axis_index("bl")
    z, xl = here // NX, here % NX
    fx = facet // FGRID * cells
    fy = facet % FGRID * cells
    own = screens.shape[1]
    lanes = cells // wide
    narrow = jnp.bfloat16

    def zshift(value, by):
        pairs = [(a * NX + b, (a + by) % nz * NX + b) for a in range(nz) for b in range(NX)]
        return lax.ppermute(value, "bl", pairs)

    def swap(value):
        return lax.ppermute(value, "bl", [(i, i ^ 1) for i in range(bl)])

    def fswap(value, bit):
        return lax.ppermute(value, "facet", [(i, i ^ bit) for i in range(nf)])

    place = jnp.stack([here, facet % 2]).astype(jnp.int32)

    block = jnp.concatenate(
        [facet_model[0].reshape(rows, lanes, wide).transpose(1, 0, 2), screens[0]], axis=0
    )
    up1, down1 = zshift(block, 1), zshift(block, -1)
    both = jnp.concatenate([offsets, stations], axis=0)
    both_far = swap(both)
    offs = jnp.concatenate([both[:tiles], both_far[:tiles]], axis=0)

    spot = jnp.arange(cells // NX, dtype=jnp.int32)
    pixel_u = fx + ((z + spot // rows) % nz * NX + xl) * rows + spot % rows
    pixel_v = fy + jnp.arange(cells, dtype=jnp.int32)
    cell = jnp.arange(width, dtype=jnp.int32)
    eu_c, eu_s = wave(cell, pixel_u, grid)
    ou_c, ou_s = wave(offs[:, 0], pixel_u, grid)
    ev_c, ev_s = wave(cell, pixel_v, grid)
    ov_c, ov_s = wave(offs[:, 1], pixel_v, grid)
    eu_1 = jnp.concatenate([eu_c, -eu_s], axis=0)
    eu_2 = jnp.concatenate([-eu_s, -eu_c], axis=0)
    ev_1 = jnp.concatenate([ev_c, ev_s], axis=0)
    ev_2 = jnp.concatenate([-ev_s, ev_c], axis=0)
    tab_u = (ou_c[:, None] * eu_1[None] + ou_s[:, None] * eu_2[None]).astype(narrow)
    tab_v = (ov_c[:, None] * ev_1[None] + ov_s[:, None] * ev_2[None]).astype(narrow)

    up2, down2 = zshift(up1, 1), zshift(down1, -1)
    up3, down3 = zshift(up2, 1), zshift(down2, -1)
    half = block.shape[0] // 2
    first, second = zshift(up3[:half], 1), zshift(down3[half:], -1)

    relative = [block, down1, down2, down3, first, up3, up2, up1]
    other = swap(predict_call("predict_far", tab_u, tab_v, relative, narrow, tiles, tiles, 4))

    gains = relative + [second]
    (x,) = gain_call(
        far_gain_kernel, "gain_far", own, nz, place, both_far, [], gains, [(tiles, narrow)], tiles
    )
    x = swap(x)
    s = predict_call("predict_own", tab_u, tab_v, relative, jnp.float32, 0, tiles, 4)
    part = tiles // 2
    wides = [(count, jnp.float32) for count in (tiles, part, part)]
    gain, keep, give = gain_call(
        own_gain_kernel, "gain_own", own, nz, place, both, [x, s, other], gains, wides, tiles
    )

    keep = keep + fswap(give, 1)
    bit = 2
    while bit < nf:
        sent = keep.astype(narrow)
        keep = sent.astype(jnp.float32) + fswap(sent, bit).astype(jnp.float32)
        bit *= 2
    others = fswap(keep, 1)
    residual, w = pl.pallas_call(
        residual_kernel,
        out_shape=[
            jax.ShapeDtypeStruct(observed.shape, jnp.float32),
            jax.ShapeDtypeStruct(observed.shape, narrow),
        ],
        in_specs=[pl.BlockSpec(memory_space=pltpu.SMEM)] * 2
        + [pl.BlockSpec(memory_space=pltpu.VMEM)] * 4,
        out_specs=[pl.BlockSpec(memory_space=pltpu.VMEM)] * 2,
        name="residual",
    )(place, counts, keep, others, observed, gain)
    def grid_rows(w, tab_v):
        w_re, w_im = w[..., :width], w[..., width:]
        stacked = jnp.concatenate(
            [jnp.concatenate([w_re, -w_im], axis=2), jnp.concatenate([w_im, w_re], axis=2)], axis=1
        )
        return jnp.einsum(
            "tuk,tky->tuy", stacked, tab_v, preferred_element_type=jnp.float32
        ).astype(narrow)

    w_far = swap(w)
    q_own = grid_rows(w, tab_v[:tiles])
    q_far = grid_rows(w_far, tab_v[tiles:])

    def image(low, high):
        return sum(
            jnp.einsum(
                "tkx,tky->xy",
                tab_u[at : at + tiles, :, low * rows : high * rows],
                q,
                preferred_element_type=jnp.float32,
            )
            for at, q in ((0, q_own), (tiles, q_far))
        )

    outer = image(2, 6).reshape(4, rows, cells)
    cut = rows // 2
    opposite = outer[2].astype(narrow)
    a, b = zshift(opposite[:cut], 1), zshift(opposite[cut:], -1)
    inner = jnp.concatenate([image(6, 8), image(0, 2)], axis=0).reshape(4, rows, cells)
    up = jnp.concatenate([outer[1][:cut] + a.astype(jnp.float32), outer[1][cut:]], axis=0)
    down = jnp.concatenate([outer[3][:cut], outer[3][cut:] + b.astype(jnp.float32)], axis=0)
    for add_up, add_down in ((outer[0], inner[0]), (inner[3], inner[1])):
        up = add_up + zshift(up.astype(narrow), 1).astype(jnp.float32)
        down = add_down + zshift(down.astype(narrow), -1).astype(jnp.float32)
    up, down = zshift(up.astype(narrow), 1), zshift(down.astype(narrow), -1)
    scale = 1.0 / (32.0 * width * math.sqrt(tiles * bl))
    own_rows = inner[2] + up.astype(jnp.float32) + down.astype(jnp.float32)
    return (residual, (own_rows * scale)[None])


def solution(mesh):
    in_specs = (
        P("facet", "bl", None),
        P("facet", "bl", None, None),
        P("bl", None, None),
        P("bl", None),
        P("bl", None),
        P("bl"),
    )
    out_specs = (P("bl", None, None), P("facet", "bl", None))
    return jax.shard_map(
        per_device, mesh=mesh, in_specs=in_specs, out_specs=out_specs, check_vma=False
    )
```

```python
import functools
import math

import jax
import jax.numpy as jnp
from jax import lax
from jax.experimental import pallas as pl
from jax.experimental.pallas import tpu as pltpu
from jax.sharding import PartitionSpec as P

FGRID = 4
NX = 2


def wave(count, pixel, cells):
    turn = jnp.mod(count[:, None] * pixel[None, :], cells)
    angle = turn.astype(jnp.float32) * (2.0 * math.pi / cells)
    return jnp.cos(angle), jnp.sin(angle)


def times(a, b):
    half = a.shape[-1] // 2
    turned = pltpu.roll(b, half, 1)
    same, cross = a * b, a * turned
    real = lax.broadcasted_iota(jnp.int32, a.shape, 1) < half
    return jnp.where(real, same - pltpu.roll(same, half, 1), cross + pltpu.roll(cross, half, 1))


def times_conj(a, b):
    half = a.shape[-1] // 2
    turned = pltpu.roll(b, half, 1)
    same, cross = a * b, a * turned
    real = lax.broadcasted_iota(jnp.int32, a.shape, 1) < half
    return jnp.where(real, same + pltpu.roll(same, half, 1), cross - pltpu.roll(cross, half, 1))


def room(mib):
    return pltpu.CompilerParams(vmem_limit_bytes=mib << 20)


def split(number, by):
    if by & (by - 1) == 0:
        return lax.shift_right_logical(number, by.bit_length() - 1), number & (by - 1)
    return number // by, lax.rem(number, by)


def pack_kernel(model_ref, screens_ref, out_ref, sems):
    wide = out_ref.shape[2]
    lanes = model_ref.shape[2] // wide
    own = screens_ref.shape[1]
    copies = [
        pltpu.make_async_copy(
            model_ref.at[0, :, pl.ds(lane * wide, wide)], out_ref.at[lane], sems.at[lane]
        )
        for lane in range(lanes)
    ]
    copies.append(
        pltpu.make_async_copy(screens_ref.at[0], out_ref.at[pl.ds(lanes, own)], sems.at[lanes])
    )
    for copy in copies:
        copy.start()
    for copy in copies:
        copy.wait()


def pack(model, screens):
    own, width, wide = screens.shape[1:]
    lanes = model.shape[2] // wide
    return pl.pallas_call(
        pack_kernel,
        out_shape=jax.ShapeDtypeStruct((lanes + own, width, wide), model.dtype),
        in_specs=[pl.BlockSpec(memory_space=pl.ANY)] * 2,
        out_specs=pl.BlockSpec(memory_space=pltpu.VMEM),
        scratch_shapes=[pltpu.SemaphoreType.DMA((lanes + 1,))],
        compiler_params=room(2),
        name="pack",
    )(model, screens)


def picked_gain(place_ref, station_ref, pool, tile, tiles, own, nz):
    z, xl = split(place_ref[0], NX)
    lane = lax.broadcasted_iota(jnp.int32, pool.shape[1:], 1)
    one = (lane < pool.shape[2] // 2).astype(jnp.float32)
    found = []
    for side in range(2):
        owner, row = split(station_ref[tiles + tile, side], own)
        owner_z, owner_xl = split(owner, NX)
        away = split(owner_z - z + nz, nz)[1]
        here = (owner_xl == xl).astype(jnp.float32)
        found.append(pool[away * own + row].astype(jnp.float32) * here + one * (1.0 - here))
    return times_conj(*found)


def far_gain_kernel(own, nz, place_ref, station_ref, *refs):
    *blocks, x_ref, pool = refs
    tiles = x_ref.shape[0]
    skip = blocks[0].shape[0] - own
    at = 0
    for number, block in enumerate(blocks):
        lead = 0 if number == nz // 2 + 1 else skip
        count = block.shape[0] - lead
        pool[at : at + count] = block[lead:]
        at += count
    for tile in range(tiles):
        value = picked_gain(place_ref, station_ref, pool, tile, tiles, own, nz)
        x_ref[tile] = value.astype(x_ref.dtype)


def own_gain_kernel(own, nz, place_ref, station_ref, *refs):
    pool, x_ref, s_ref, other_ref, gain_ref, keep_ref, give_ref = refs
    tiles = x_ref.shape[0]
    part = tiles // 2
    core = place_ref[1]
    lead = lax.broadcasted_iota(jnp.int32, s_ref.shape[1:], 0) >= core * s_ref.shape[1]

    def sums(tile):
        gain = picked_gain(place_ref, station_ref, pool, tile, tiles, own, nz)
        gain = times(gain, x_ref[tile].astype(jnp.float32))
        gain_ref[tile] = gain
        return times(gain, s_ref[tile] + other_ref[tile].astype(jnp.float32))

    for tile in range(part):
        low, high = sums(tile), sums(tile + part)
        keep_ref[tile] = jnp.where(lead, low, high)
        give_ref[tile] = jnp.where(lead, high, low)


def gain_call(kernel, name, own, nz, place, stations, dense, outs):
    shape = dense[0].shape[1:]
    return pl.pallas_call(
        functools.partial(kernel, own, nz),
        out_shape=[jax.ShapeDtypeStruct((count,) + shape, kind) for count, kind in outs],
        in_specs=[pl.BlockSpec(memory_space=pltpu.SMEM)] * 2
        + [pl.BlockSpec(memory_space=pltpu.VMEM)] * len(dense),
        out_specs=[pl.BlockSpec(memory_space=pltpu.VMEM)] * len(outs),
        compiler_params=room(12),
        name=name,
    )(place, stations, *dense)


def predict_kernel(u_ref, v_ref, *refs):
    *blocks, s_ref, model = refs
    rows = blocks[0].shape[1]
    wide = blocks[0].shape[2]

    @pl.when(pl.program_id(0) == 0)
    def _():
        for number, block in enumerate(blocks):
            for lane in range(model.shape[1] // wide):
                model[number * rows : (number + 1) * rows, lane * wide : (lane + 1) * wide] = block[
                    lane
                ]

    count, height, deep = u_ref.shape
    upper = jnp.dot(
        u_ref[...].reshape(count * height, deep), model[...], preferred_element_type=jnp.float32
    ).astype(jnp.bfloat16)
    half = height // 2
    for tile in range(count):
        both = lax.dot_general(
            upper[tile * height : (tile + 1) * height],
            v_ref[tile],
            (((1,), (1,)), ((), ())),
            preferred_element_type=jnp.float32,
        )
        top, low = both[:half], pltpu.roll(both[half:], half, 1)
        real = lax.broadcasted_iota(jnp.int32, top.shape, 1) < half
        s_ref[tile] = jnp.where(real, top + low, low - top).astype(s_ref.dtype)


def predict_call(name, tab_u, tab_v, blocks, kind, first, tiles, step):
    height, deep = tab_u.shape[1:]
    cells = tab_v.shape[2]
    rows, wide = blocks[0].shape[1:]
    lanes = cells // wide
    begin = first // step
    return pl.pallas_call(
        predict_kernel,
        grid=(tiles // step,),
        out_shape=jax.ShapeDtypeStruct((tiles, height // 2, height), kind),
        in_specs=[
            pl.BlockSpec((step, height, deep), lambda i: (begin + i, 0, 0)),
            pl.BlockSpec((step, height, cells), lambda i: (begin + i, 0, 0)),
        ]
        + [pl.BlockSpec((lanes, rows, wide), lambda i: (0, 0, 0))] * len(blocks),
        out_specs=pl.BlockSpec((step, height // 2, height), lambda i: (i, 0, 0)),
        scratch_shapes=[pltpu.VMEM((deep, cells), tab_u.dtype)],
        compiler_params=room(20),
        name=name,
    )(tab_u, tab_v, *blocks)


def residual_kernel(place_ref, count_ref, keep_ref, others_ref, seen_ref, gain_ref, res_ref, w_ref):
    tiles = seen_ref.shape[0]
    part = tiles // 2
    core = place_ref[1]
    count = count_ref[0]
    for tile in range(tiles):
        live = (tile < count).astype(jnp.int32)
        mine = (core == tile // part).astype(jnp.float32)
        value = keep_ref[tile % part] * mine + others_ref[tile % part] * (1.0 - mine)
        alive = lax.broadcasted_iota(jnp.int32, value.shape, 0) >= (1 - live) * value.shape[0]
        value = jnp.where(alive, seen_ref[tile] - value, 0.0)
        res_ref[tile] = value
        w_ref[tile] = times_conj(value, gain_ref[tile]).astype(w_ref.dtype)


def fold_kernel(up_at, down_at, a_ref, b_ref, up_ref, down_ref, up_out, down_out):
    some = a_ref.shape[0]
    for at, came, mine, out in ((up_at, a_ref, up_ref, up_out), (down_at, b_ref, down_ref, down_out)):
        for row in range(0, mine.shape[0], some):
            value = mine[row : row + some]
            if row == at:
                value = value + came[...].astype(jnp.float32)
            out[row : row + some] = value.astype(out.dtype)


def fold(a, b, up, down, up_at=0, down_at=0):
    return pl.pallas_call(
        functools.partial(fold_kernel, up_at, down_at),
        out_shape=[jax.ShapeDtypeStruct(up.shape, a.dtype)] * 2,
        in_specs=[pl.BlockSpec(memory_space=pltpu.VMEM)] * 4,
        out_specs=[pl.BlockSpec(memory_space=pltpu.VMEM)] * 2,
        compiler_params=room(4),
        name="fold",
    )(a, b, up, down)


def per_device(facet_model, screens, observed, offsets, stations, counts):
    tiles, width, wide = observed.shape
    cells = facet_model.shape[2]
    rows = facet_model.shape[1]
    bl = lax.axis_size("bl")
    nz = bl // NX
    nf = lax.axis_size("facet")
    grid = FGRID * cells
    facet = lax.axis_index("facet")
    here = lax.axis_index("bl")
    z, xl = here // NX, here % NX
    fx = facet // FGRID * cells
    fy = facet % FGRID * cells
    own = screens.shape[1]
    lanes = cells // wide
    narrow = jnp.bfloat16

    def zshift(value, by):
        pairs = [(a * NX + b, (a + by) % nz * NX + b) for a in range(nz) for b in range(NX)]
        return lax.ppermute(value, "bl", pairs)

    def swap(value):
        return lax.ppermute(value, "bl", [(i, i ^ 1) for i in range(bl)])

    def fswap(value, bit):
        return lax.ppermute(value, "facet", [(i, i ^ bit) for i in range(nf)])

    place = jnp.stack([here, facet % 2]).astype(jnp.int32)

    block = pack(facet_model, screens)
    up1, down1 = zshift(block, 1), zshift(block, -1)
    both = jnp.concatenate([offsets, stations], axis=0)
    both_far = swap(both)
    offs = jnp.concatenate([both[:tiles], both_far[:tiles]], axis=0)

    spot = jnp.arange(cells // NX, dtype=jnp.int32)
    pixel_u = fx + ((z + spot // rows) % nz * NX + xl) * rows + spot % rows
    pixel_v = fy + jnp.arange(cells, dtype=jnp.int32)
    cell = jnp.arange(width, dtype=jnp.int32)
    eu_c, eu_s = wave(cell, pixel_u, grid)
    ou_c, ou_s = wave(offs[:, 0], pixel_u, grid)
    ev_c, ev_s = wave(cell, pixel_v, grid)
    ov_c, ov_s = wave(offs[:, 1], pixel_v, grid)
    eu_1 = jnp.concatenate([eu_c, -eu_s], axis=0)
    eu_2 = jnp.concatenate([-eu_s, -eu_c], axis=0)
    ev_1 = jnp.concatenate([ev_c, ev_s], axis=0)
    ev_2 = jnp.concatenate([-ev_s, ev_c], axis=0)
    tab_u = (ou_c[:, None] * eu_1[None] + ou_s[:, None] * eu_2[None]).astype(narrow)
    tab_v = (ov_c[:, None] * ev_1[None] + ov_s[:, None] * ev_2[None]).astype(narrow)

    up2, down2 = zshift(up1, 1), zshift(down1, -1)
    up3, down3 = zshift(up2, 1), zshift(down2, -1)
    half = block.shape[0] // 2
    first, second = zshift(up3[:half], 1), zshift(down3[half:], -1)

    relative = [block, down1, down2, down3, first, up3, up2, up1]
    other = swap(predict_call("predict_far", tab_u, tab_v, relative, narrow, tiles, tiles, 4))

    gains = relative[: nz // 2 + 1] + [second] + relative[nz // 2 + 1 :]
    slim = [(tiles, narrow), (nz * own, narrow)]
    x, pool = gain_call(far_gain_kernel, "gain_far", own, nz, place, both_far, gains, slim)
    x = swap(x)
    s = predict_call("predict_own", tab_u, tab_v, relative, jnp.float32, 0, tiles, 4)
    part = tiles // 2
    wides = [(count, jnp.float32) for count in (tiles, part, part)]
    gain, keep, give = gain_call(
        own_gain_kernel, "gain_own", own, nz, place, both, [pool, x, s, other], wides
    )

    keep = keep + fswap(give, 1)
    bit = 2
    while bit < nf:
        sent = keep.astype(narrow)
        keep = sent.astype(jnp.float32) + fswap(sent, bit).astype(jnp.float32)
        bit *= 2
    others = fswap(keep, 1)
    residual, w = pl.pallas_call(
        residual_kernel,
        out_shape=[
            jax.ShapeDtypeStruct(observed.shape, jnp.float32),
            jax.ShapeDtypeStruct(observed.shape, narrow),
        ],
        in_specs=[pl.BlockSpec(memory_space=pltpu.SMEM)] * 2
        + [pl.BlockSpec(memory_space=pltpu.VMEM)] * 4,
        out_specs=[pl.BlockSpec(memory_space=pltpu.VMEM)] * 2,
        compiler_params=room(8),
        name="residual",
    )(place, counts, keep, others, observed, gain)
    def grid_rows(w, tab_v):
        w_re, w_im = w[..., :width], w[..., width:]
        stacked = jnp.concatenate(
            [jnp.concatenate([w_re, -w_im], axis=2), jnp.concatenate([w_im, w_re], axis=2)], axis=1
        )
        return jnp.einsum(
            "tuk,tky->tuy", stacked, tab_v, preferred_element_type=jnp.float32
        ).astype(narrow)

    def image(at, q, low, high):
        return jnp.einsum(
            "tkx,tky->xy",
            tab_u[at : at + tiles, :, low * rows : high * rows],
            q,
            preferred_element_type=jnp.float32,
        )

    def after(value, other):
        return value + jnp.minimum(jnp.abs(other[0, 0]), 0.0).astype(value.dtype)

    w_far = swap(w)
    q_own = grid_rows(w, tab_v[:tiles])
    spans = ((2, 6), (6, 8), (0, 2))
    owns = [image(0, q_own, *span) for span in spans]
    q_far = grid_rows(after(w_far, owns[0]), tab_v[tiles:])
    outer, late, early = (a + image(tiles, q_far, *span) for a, span in zip(owns, spans))

    outer = outer.reshape(4, rows, cells)
    cut = rows // 2
    opposite = outer[2].astype(narrow)
    a, b = zshift(opposite[:cut], 1), zshift(opposite[cut:], -1)
    inner = jnp.concatenate([late, early], axis=0).reshape(4, rows, cells)
    up, down = fold(a, b, outer[1], outer[3], 0, cut)
    for add_up, add_down in ((outer[0], inner[0]), (inner[3], inner[1])):
        up, down = fold(zshift(up, 1), zshift(down, -1), add_up, add_down)
    up, down = zshift(up, 1), zshift(down, -1)
    scale = 1.0 / (32.0 * width * math.sqrt(tiles * bl))
    own_rows = inner[2] + up.astype(jnp.float32) + down.astype(jnp.float32)
    return (residual, (own_rows * scale)[None])


def solution(mesh):
    in_specs = (
        P("facet", "bl", None),
        P("facet", "bl", None, None),
        P("bl", None, None),
        P("bl", None),
        P("bl", None),
        P("bl"),
    )
    out_specs = (P("bl", None, None), P("facet", "bl", None))
    return jax.shard_map(
        per_device, mesh=mesh, in_specs=in_specs, out_specs=out_specs, check_vma=False
    )
```

```python
import functools
import math

import jax
import jax.numpy as jnp
from jax import lax
from jax.experimental import pallas as pl
from jax.experimental.pallas import tpu as pltpu
from jax.sharding import PartitionSpec as P

FGRID = 4
NX = 2


def wave(count, pixel, cells):
    turn = jnp.mod(count[:, None] * pixel[None, :], cells)
    angle = turn.astype(jnp.float32) * (2.0 * math.pi / cells)
    return jnp.cos(angle), jnp.sin(angle)


def times(a, b):
    half = a.shape[-1] // 2
    turned = pltpu.roll(b, half, 1)
    same, cross = a * b, a * turned
    real = lax.broadcasted_iota(jnp.int32, a.shape, 1) < half
    return jnp.where(real, same - pltpu.roll(same, half, 1), cross + pltpu.roll(cross, half, 1))


def times_conj(a, b):
    half = a.shape[-1] // 2
    turned = pltpu.roll(b, half, 1)
    same, cross = a * b, a * turned
    real = lax.broadcasted_iota(jnp.int32, a.shape, 1) < half
    return jnp.where(real, same + pltpu.roll(same, half, 1), cross - pltpu.roll(cross, half, 1))


def room(mib):
    return pltpu.CompilerParams(vmem_limit_bytes=mib << 20)


def split(number, by):
    if by & (by - 1) == 0:
        return lax.shift_right_logical(number, by.bit_length() - 1), number & (by - 1)
    return number // by, lax.rem(number, by)


def pack_kernel(model_ref, screens_ref, out_ref, sems):
    wide = out_ref.shape[2]
    lanes = model_ref.shape[2] // wide
    own = screens_ref.shape[1]
    copies = [
        pltpu.make_async_copy(
            model_ref.at[0, :, pl.ds(lane * wide, wide)], out_ref.at[lane], sems.at[lane]
        )
        for lane in range(lanes)
    ]
    copies.append(
        pltpu.make_async_copy(screens_ref.at[0], out_ref.at[pl.ds(lanes, own)], sems.at[lanes])
    )
    for copy in copies:
        copy.start()
    for copy in copies:
        copy.wait()


def pack(model, screens):
    own, width, wide = screens.shape[1:]
    lanes = model.shape[2] // wide
    return pl.pallas_call(
        pack_kernel,
        out_shape=jax.ShapeDtypeStruct((lanes + own, width, wide), model.dtype),
        in_specs=[pl.BlockSpec(memory_space=pltpu.HBM)] * 2,
        out_specs=pl.BlockSpec(memory_space=pltpu.VMEM),
        scratch_shapes=[pltpu.SemaphoreType.DMA((lanes + 1,))],
        compiler_params=room(2),
        name="pack",
    )(model, screens)


def picked_gain(place_ref, station_ref, pool, tile, tiles, own, nz):
    z, xl = split(place_ref[0], NX)
    lane = lax.broadcasted_iota(jnp.int32, pool.shape[1:], 1)
    one = (lane < pool.shape[2] // 2).astype(jnp.float32)
    found = []
    for side in range(2):
        owner, row = split(station_ref[tiles + tile, side], own)
        owner_z, owner_xl = split(owner, NX)
        away = split(owner_z - z + nz, nz)[1]
        here = (owner_xl == xl).astype(jnp.float32)
        found.append(pool[away * own + row].astype(jnp.float32) * here + one * (1.0 - here))
    return times_conj(*found)


def far_gain_kernel(own, nz, place_ref, station_ref, *refs):
    *blocks, x_ref, pool = refs
    tiles = x_ref.shape[0]
    skip = blocks[0].shape[0] - own
    at = 0
    for number, block in enumerate(blocks):
        lead = 0 if number == nz // 2 + 1 else skip
        count = block.shape[0] - lead
        pool[at : at + count] = block[lead:]
        at += count
    for tile in range(tiles):
        value = picked_gain(place_ref, station_ref, pool, tile, tiles, own, nz)
        x_ref[tile] = value.astype(x_ref.dtype)


def own_gain_kernel(own, nz, place_ref, station_ref, *refs):
    pool, x_ref, s_ref, other_ref, gain_ref, keep_ref, give_ref = refs
    tiles = x_ref.shape[0]
    part = tiles // 2
    core = place_ref[1]
    lead = lax.broadcasted_iota(jnp.int32, s_ref.shape[1:], 0) >= core * s_ref.shape[1]

    def sums(tile):
        gain = picked_gain(place_ref, station_ref, pool, tile, tiles, own, nz)
        gain = times(gain, x_ref[tile].astype(jnp.float32))
        gain_ref[tile] = gain
        return times(gain, s_ref[tile] + other_ref[tile].astype(jnp.float32))

    for tile in range(part):
        low, high = sums(tile), sums(tile + part)
        keep_ref[tile] = jnp.where(lead, low, high)
        give_ref[tile] = jnp.where(lead, high, low)


def gain_call(kernel, name, own, nz, place, stations, dense, outs):
    shape = dense[0].shape[1:]
    return pl.pallas_call(
        functools.partial(kernel, own, nz),
        out_shape=[jax.ShapeDtypeStruct((count,) + shape, kind) for count, kind in outs],
        in_specs=[pl.BlockSpec(memory_space=pltpu.SMEM)] * 2
        + [pl.BlockSpec(memory_space=pltpu.VMEM)] * len(dense),
        out_specs=[pl.BlockSpec(memory_space=pltpu.VMEM)] * len(outs),
        compiler_params=room(12),
        name=name,
    )(place, stations, *dense)


def predict_kernel(u_ref, v_ref, *refs):
    *blocks, s_ref, model = refs
    rows = blocks[0].shape[1]
    wide = blocks[0].shape[2]

    @pl.when(pl.program_id(0) == 0)
    def _():
        for number, block in enumerate(blocks):
            for lane in range(model.shape[1] // wide):
                model[number * rows : (number + 1) * rows, lane * wide : (lane + 1) * wide] = block[
                    lane
                ]

    count, height, deep = u_ref.shape
    upper = jnp.dot(
        u_ref[...].reshape(count * height, deep), model[...], preferred_element_type=jnp.float32
    ).astype(jnp.bfloat16)
    half = height // 2
    for tile in range(count):
        both = lax.dot_general(
            upper[tile * height : (tile + 1) * height],
            v_ref[tile],
            (((1,), (1,)), ((), ())),
            preferred_element_type=jnp.float32,
        )
        top, low = both[:half], pltpu.roll(both[half:], half, 1)
        real = lax.broadcasted_iota(jnp.int32, top.shape, 1) < half
        s_ref[tile] = jnp.where(real, top + low, low - top).astype(s_ref.dtype)


def predict_call(name, tab_u, tab_v, blocks, kind, first, tiles, step):
    height, deep = tab_u.shape[1:]
    cells = tab_v.shape[2]
    rows, wide = blocks[0].shape[1:]
    lanes = cells // wide
    begin = first // step
    return pl.pallas_call(
        predict_kernel,
        grid=(tiles // step,),
        out_shape=jax.ShapeDtypeStruct((tiles, height // 2, height), kind),
        in_specs=[
            pl.BlockSpec((step, height, deep), lambda i: (begin + i, 0, 0)),
            pl.BlockSpec((step, height, cells), lambda i: (begin + i, 0, 0)),
        ]
        + [pl.BlockSpec((lanes, rows, wide), lambda i: (0, 0, 0))] * len(blocks),
        out_specs=pl.BlockSpec((step, height // 2, height), lambda i: (i, 0, 0)),
        scratch_shapes=[pltpu.VMEM((deep, cells), tab_u.dtype)],
        compiler_params=room(20),
        name=name,
    )(tab_u, tab_v, *blocks)


def residual_kernel(place_ref, count_ref, keep_ref, others_ref, seen_ref, gain_ref, res_ref, w_ref):
    tiles = seen_ref.shape[0]
    part = tiles // 2
    core = place_ref[1]
    count = count_ref[0]
    for tile in range(tiles):
        live = (tile < count).astype(jnp.int32)
        mine = (core == tile // part).astype(jnp.float32)
        value = keep_ref[tile % part] * mine + others_ref[tile % part] * (1.0 - mine)
        alive = lax.broadcasted_iota(jnp.int32, value.shape, 0) >= (1 - live) * value.shape[0]
        value = jnp.where(alive, seen_ref[tile] - value, 0.0)
        res_ref[tile] = value
        w_ref[tile] = times_conj(value, gain_ref[tile]).astype(w_ref.dtype)


def fold_kernel(up_at, down_at, a_ref, b_ref, up_ref, down_ref, up_out, down_out):
    some = a_ref.shape[0]
    for at, came, mine, out in ((up_at, a_ref, up_ref, up_out), (down_at, b_ref, down_ref, down_out)):
        for row in range(0, mine.shape[0], some):
            value = mine[row : row + some]
            if row == at:
                value = value + came[...].astype(jnp.float32)
            out[row : row + some] = value.astype(out.dtype)


def fold(a, b, up, down, up_at=0, down_at=0):
    return pl.pallas_call(
        functools.partial(fold_kernel, up_at, down_at),
        out_shape=[jax.ShapeDtypeStruct(up.shape, a.dtype)] * 2,
        in_specs=[pl.BlockSpec(memory_space=pltpu.VMEM)] * 4,
        out_specs=[pl.BlockSpec(memory_space=pltpu.VMEM)] * 2,
        compiler_params=room(4),
        name="fold",
    )(a, b, up, down)


def per_device(facet_model, screens, observed, offsets, stations, counts):
    tiles, width, wide = observed.shape
    cells = facet_model.shape[2]
    rows = facet_model.shape[1]
    bl = lax.axis_size("bl")
    nz = bl // NX
    nf = lax.axis_size("facet")
    grid = FGRID * cells
    facet = lax.axis_index("facet")
    here = lax.axis_index("bl")
    z, xl = here // NX, here % NX
    fx = facet // FGRID * cells
    fy = facet % FGRID * cells
    own = screens.shape[1]
    lanes = cells // wide
    narrow = jnp.bfloat16

    def zshift(value, by):
        pairs = [(a * NX + b, (a + by) % nz * NX + b) for a in range(nz) for b in range(NX)]
        return lax.ppermute(value, "bl", pairs)

    def swap(value):
        return lax.ppermute(value, "bl", [(i, i ^ 1) for i in range(bl)])

    def fswap(value, bit):
        return lax.ppermute(value, "facet", [(i, i ^ bit) for i in range(nf)])

    place = jnp.stack([here, facet % 2]).astype(jnp.int32)

    block = pack(
        pltpu.with_memory_space_constraint(facet_model, pltpu.HBM),
        pltpu.with_memory_space_constraint(screens, pltpu.HBM),
    )
    up1, down1 = zshift(block, 1), zshift(block, -1)
    both = jnp.concatenate([offsets, stations], axis=0)
    both_far = swap(both)
    offs = jnp.concatenate([both[:tiles], both_far[:tiles]], axis=0)

    spot = jnp.arange(cells // NX, dtype=jnp.int32)
    pixel_u = fx + ((z + spot // rows) % nz * NX + xl) * rows + spot % rows
    pixel_v = fy + jnp.arange(cells, dtype=jnp.int32)
    cell = jnp.arange(width, dtype=jnp.int32)
    eu_c, eu_s = wave(cell, pixel_u, grid)
    ou_c, ou_s = wave(offs[:, 0], pixel_u, grid)
    ev_c, ev_s = wave(cell, pixel_v, grid)
    ov_c, ov_s = wave(offs[:, 1], pixel_v, grid)
    eu_1 = jnp.concatenate([eu_c, -eu_s], axis=0)
    eu_2 = jnp.concatenate([-eu_s, -eu_c], axis=0)
    ev_1 = jnp.concatenate([ev_c, ev_s], axis=0)
    ev_2 = jnp.concatenate([-ev_s, ev_c], axis=0)
    tab_u = (ou_c[:, None] * eu_1[None] + ou_s[:, None] * eu_2[None]).astype(narrow)
    tab_v = (ov_c[:, None] * ev_1[None] + ov_s[:, None] * ev_2[None]).astype(narrow)

    up2, down2 = zshift(up1, 1), zshift(down1, -1)
    up3, down3 = zshift(up2, 1), zshift(down2, -1)
    half = block.shape[0] // 2
    first, second = zshift(up3[:half], 1), zshift(down3[half:], -1)

    relative = [block, down1, down2, down3, first, up3, up2, up1]
    other = swap(predict_call("predict_far", tab_u, tab_v, relative, narrow, tiles, tiles, 4))

    gains = relative[: nz // 2 + 1] + [second] + relative[nz // 2 + 1 :]
    slim = [(tiles, narrow), (nz * own, narrow)]
    x, pool = gain_call(far_gain_kernel, "gain_far", own, nz, place, both_far, gains, slim)
    x = swap(x)
    s = predict_call("predict_own", tab_u, tab_v, relative, jnp.float32, 0, tiles, 4)
    part = tiles // 2
    wides = [(count, jnp.float32) for count in (tiles, part, part)]
    gain, keep, give = gain_call(
        own_gain_kernel, "gain_own", own, nz, place, both, [pool, x, s, other], wides
    )

    keep = keep + fswap(give, 1)
    for bit in (2, 4, 12):
        sent = keep.astype(narrow)
        keep = sent.astype(jnp.float32) + fswap(sent, bit).astype(jnp.float32)
    others = fswap(keep, 1)
    residual, w = pl.pallas_call(
        residual_kernel,
        out_shape=[
            jax.ShapeDtypeStruct(observed.shape, jnp.float32),
            jax.ShapeDtypeStruct(observed.shape, narrow),
        ],
        in_specs=[pl.BlockSpec(memory_space=pltpu.SMEM)] * 2
        + [pl.BlockSpec(memory_space=pltpu.VMEM)] * 4,
        out_specs=[pl.BlockSpec(memory_space=pltpu.VMEM)] * 2,
        compiler_params=room(8),
        name="residual",
    )(place, counts, keep, others, observed, gain)
    def grid_rows(w, tab_v):
        w_re, w_im = w[..., :width], w[..., width:]
        stacked = jnp.concatenate(
            [jnp.concatenate([w_re, -w_im], axis=2), jnp.concatenate([w_im, w_re], axis=2)], axis=1
        )
        return jnp.einsum(
            "tuk,tky->tuy", stacked, tab_v, preferred_element_type=jnp.float32
        ).astype(narrow)

    def image(at, q, low, high):
        return jnp.einsum(
            "tkx,tky->xy",
            tab_u[at : at + tiles, :, low * rows : high * rows],
            q,
            preferred_element_type=jnp.float32,
        )

    def after(value, other):
        return value + jnp.minimum(jnp.abs(other[0, 0]), 0.0).astype(value.dtype)

    w_far = swap(w)
    q_own = grid_rows(w, tab_v[:tiles])
    spans = ((2, 7), (7, 8), (0, 2))
    owns = [image(0, q_own, *span) for span in spans]
    q_far = grid_rows(after(w_far, owns[0]), tab_v[tiles:])
    outer = (owns[0] + image(tiles, q_far, *spans[0])).reshape(5, rows, cells)

    cut = rows // 2
    opposite = outer[2].astype(narrow)
    a, b = zshift(opposite[:cut], 1), zshift(opposite[cut:], -1)
    q_late = after(q_far, a)
    inner = [mine + image(tiles, q_late, *span) for mine, span in zip(owns[1:], spans[1:])]
    inner = jnp.concatenate(inner, axis=0).reshape(3, rows, cells)
    up, down = fold(a, b, outer[1], outer[3], 0, cut)
    for add_up, add_down in ((outer[0], outer[4]), (inner[2], inner[0])):
        up, down = fold(zshift(up, 1), zshift(down, -1), add_up, add_down)
    up, down = zshift(up, 1), zshift(down, -1)
    scale = 1.0 / (32.0 * width * math.sqrt(tiles * bl))
    own_rows = inner[1] + up.astype(jnp.float32) + down.astype(jnp.float32)
    return (residual, (own_rows * scale)[None])


def solution(mesh):
    in_specs = (
        P("facet", "bl", None),
        P("facet", "bl", None, None),
        P("bl", None, None),
        P("bl", None),
        P("bl", None),
        P("bl"),
    )
    out_specs = (P("bl", None, None), P("facet", "bl", None))
    return jax.shard_map(
        per_device, mesh=mesh, in_specs=in_specs, out_specs=out_specs, check_vma=False
    )
```

```python
import functools
import math

import jax
import jax.numpy as jnp
from jax import lax
from jax.experimental import pallas as pl
from jax.experimental.pallas import tpu as pltpu
from jax.sharding import PartitionSpec as P

FGRID = 4
NX = 2


def wave(count, pixel, cells):
    turn = jnp.mod(count[:, None] * pixel[None, :], cells)
    angle = turn.astype(jnp.float32) * (2.0 * math.pi / cells)
    return jnp.cos(angle), jnp.sin(angle)


def times(a, b):
    half = a.shape[-1] // 2
    turned = pltpu.roll(b, half, 1)
    same, cross = a * b, a * turned
    real = lax.broadcasted_iota(jnp.int32, a.shape, 1) < half
    return jnp.where(real, same - pltpu.roll(same, half, 1), cross + pltpu.roll(cross, half, 1))


def times_conj(a, b):
    half = a.shape[-1] // 2
    turned = pltpu.roll(b, half, 1)
    same, cross = a * b, a * turned
    real = lax.broadcasted_iota(jnp.int32, a.shape, 1) < half
    return jnp.where(real, same + pltpu.roll(same, half, 1), cross - pltpu.roll(cross, half, 1))


def room(mib):
    return pltpu.CompilerParams(vmem_limit_bytes=mib << 20)


def split(number, by):
    if by & (by - 1) == 0:
        return lax.shift_right_logical(number, by.bit_length() - 1), number & (by - 1)
    return number // by, lax.rem(number, by)


def pack_kernel(model_ref, screens_ref, out_ref, sems):
    wide = out_ref.shape[2]
    lanes = model_ref.shape[2] // wide
    own = screens_ref.shape[1]
    copies = [
        pltpu.make_async_copy(
            model_ref.at[0, :, pl.ds(lane * wide, wide)], out_ref.at[lane], sems.at[lane]
        )
        for lane in range(lanes)
    ]
    copies.append(
        pltpu.make_async_copy(screens_ref.at[0], out_ref.at[pl.ds(lanes, own)], sems.at[lanes])
    )
    for copy in copies:
        copy.start()
    for copy in copies:
        copy.wait()


def pack(model, screens):
    own, width, wide = screens.shape[1:]
    lanes = model.shape[2] // wide
    return pl.pallas_call(
        pack_kernel,
        out_shape=jax.ShapeDtypeStruct((lanes + own, width, wide), model.dtype),
        in_specs=[pl.BlockSpec(memory_space=pltpu.HBM)] * 2,
        out_specs=pl.BlockSpec(memory_space=pltpu.VMEM),
        scratch_shapes=[pltpu.SemaphoreType.DMA((lanes + 1,))],
        compiler_params=room(2),
        name="pack",
    )(model, screens)


def picked_gain(place_ref, station_ref, pool, tile, tiles, own, nz):
    z, xl = split(place_ref[0], NX)
    lane = lax.broadcasted_iota(jnp.int32, pool.shape[1:], 1)
    one = (lane < pool.shape[2] // 2).astype(jnp.float32)
    found = []
    for side in range(2):
        owner, row = split(station_ref[tiles + tile, side], own)
        owner_z, owner_xl = split(owner, NX)
        away = split(owner_z - z + nz, nz)[1]
        here = (owner_xl == xl).astype(jnp.float32)
        found.append(pool[away * own + row].astype(jnp.float32) * here + one * (1.0 - here))
    return times_conj(*found)


def far_gain_kernel(own, nz, place_ref, station_ref, *refs):
    *blocks, x_ref, pool = refs
    tiles = x_ref.shape[0]
    skip = blocks[0].shape[0] - own
    at = 0
    for number, block in enumerate(blocks):
        lead = 0 if number == nz // 2 + 1 else skip
        count = block.shape[0] - lead
        pool[at : at + count] = block[lead:]
        at += count
    for tile in range(tiles):
        value = picked_gain(place_ref, station_ref, pool, tile, tiles, own, nz)
        x_ref[tile] = value.astype(x_ref.dtype)


def own_gain_kernel(own, nz, place_ref, station_ref, *refs):
    pool, x_ref, s_ref, other_ref, gain_ref, keep_ref, give_ref = refs
    tiles = x_ref.shape[0]
    part = tiles // 2
    core = place_ref[1]
    lead = lax.broadcasted_iota(jnp.int32, s_ref.shape[1:], 0) >= core * s_ref.shape[1]

    def sums(tile):
        gain = picked_gain(place_ref, station_ref, pool, tile, tiles, own, nz)
        gain = times(gain, x_ref[tile].astype(jnp.float32))
        gain_ref[tile] = gain
        return times(gain, s_ref[tile] + other_ref[tile].astype(jnp.float32))

    for tile in range(part):
        low, high = sums(tile), sums(tile + part)
        keep_ref[tile] = jnp.where(lead, low, high)
        give_ref[tile] = jnp.where(lead, high, low)


def gain_call(kernel, name, own, nz, place, stations, dense, outs):
    shape = dense[0].shape[1:]
    return pl.pallas_call(
        functools.partial(kernel, own, nz),
        out_shape=[jax.ShapeDtypeStruct((count,) + shape, kind) for count, kind in outs],
        in_specs=[pl.BlockSpec(memory_space=pltpu.SMEM)] * 2
        + [pl.BlockSpec(memory_space=pltpu.VMEM)] * len(dense),
        out_specs=[pl.BlockSpec(memory_space=pltpu.VMEM)] * len(outs),
        compiler_params=room(12),
        name=name,
    )(place, stations, *dense)


def predict_kernel(u_ref, v_ref, *refs):
    *blocks, s_ref, model = refs
    rows = blocks[0].shape[1]
    wide = blocks[0].shape[2]

    @pl.when(pl.program_id(0) == 0)
    def _():
        for number, block in enumerate(blocks):
            for lane in range(model.shape[1] // wide):
                model[number * rows : (number + 1) * rows, lane * wide : (lane + 1) * wide] = block[
                    lane
                ]

    count, height, deep = u_ref.shape
    upper = jnp.dot(
        u_ref[...].reshape(count * height, deep), model[...], preferred_element_type=jnp.float32
    ).astype(jnp.bfloat16)
    half = height // 2
    for tile in range(count):
        both = lax.dot_general(
            upper[tile * height : (tile + 1) * height],
            v_ref[tile],
            (((1,), (1,)), ((), ())),
            preferred_element_type=jnp.float32,
        )
        top, low = both[:half], pltpu.roll(both[half:], half, 1)
        real = lax.broadcasted_iota(jnp.int32, top.shape, 1) < half
        s_ref[tile] = jnp.where(real, top + low, low - top).astype(s_ref.dtype)


def predict_call(name, tab_u, tab_v, blocks, kind, first, tiles, step):
    height, deep = tab_u.shape[1:]
    cells = tab_v.shape[2]
    rows, wide = blocks[0].shape[1:]
    lanes = cells // wide
    begin = first // step
    return pl.pallas_call(
        predict_kernel,
        grid=(tiles // step,),
        out_shape=jax.ShapeDtypeStruct((tiles, height // 2, height), kind),
        in_specs=[
            pl.BlockSpec((step, height, deep), lambda i: (begin + i, 0, 0)),
            pl.BlockSpec((step, height, cells), lambda i: (begin + i, 0, 0)),
        ]
        + [pl.BlockSpec((lanes, rows, wide), lambda i: (0, 0, 0))] * len(blocks),
        out_specs=pl.BlockSpec((step, height // 2, height), lambda i: (i, 0, 0)),
        scratch_shapes=[pltpu.VMEM((deep, cells), tab_u.dtype)],
        compiler_params=room(20),
        name=name,
    )(tab_u, tab_v, *blocks)


def residual_kernel(place_ref, count_ref, keep_ref, others_ref, seen_ref, gain_ref, res_ref, w_ref):
    tiles = seen_ref.shape[0]
    part = tiles // 2
    core = place_ref[1]
    count = count_ref[0]
    for tile in range(tiles):
        live = (tile < count).astype(jnp.int32)
        mine = (core == tile // part).astype(jnp.float32)
        value = keep_ref[tile % part] * mine + others_ref[tile % part] * (1.0 - mine)
        alive = lax.broadcasted_iota(jnp.int32, value.shape, 0) >= (1 - live) * value.shape[0]
        value = jnp.where(alive, seen_ref[tile] - value, 0.0)
        res_ref[tile] = value
        w_ref[tile] = times_conj(value, gain_ref[tile]).astype(w_ref.dtype)


def fold_kernel(up_at, down_at, a_ref, b_ref, up_ref, down_ref, up_out, down_out):
    some = a_ref.shape[0]
    for at, came, mine, out in ((up_at, a_ref, up_ref, up_out), (down_at, b_ref, down_ref, down_out)):
        for row in range(0, mine.shape[0], some):
            value = mine[row : row + some]
            if row == at:
                value = value + came[...].astype(jnp.float32)
            out[row : row + some] = value.astype(out.dtype)


def fold(a, b, up, down, up_at=0, down_at=0):
    return pl.pallas_call(
        functools.partial(fold_kernel, up_at, down_at),
        out_shape=[jax.ShapeDtypeStruct(up.shape, a.dtype)] * 2,
        in_specs=[pl.BlockSpec(memory_space=pltpu.VMEM)] * 4,
        out_specs=[pl.BlockSpec(memory_space=pltpu.VMEM)] * 2,
        compiler_params=room(4),
        name="fold",
    )(a, b, up, down)


def per_device(facet_model, screens, observed, offsets, stations, counts):
    tiles, width, wide = observed.shape
    cells = facet_model.shape[2]
    rows = facet_model.shape[1]
    bl = lax.axis_size("bl")
    nz = bl // NX
    nf = lax.axis_size("facet")
    grid = FGRID * cells
    facet = lax.axis_index("facet")
    here = lax.axis_index("bl")
    z, xl = here // NX, here % NX
    fx = facet // FGRID * cells
    fy = facet % FGRID * cells
    own = screens.shape[1]
    lanes = cells // wide
    narrow = jnp.bfloat16

    def zshift(value, by):
        pairs = [(a * NX + b, (a + by) % nz * NX + b) for a in range(nz) for b in range(NX)]
        return lax.ppermute(value, "bl", pairs)

    def swap(value):
        return lax.ppermute(value, "bl", [(i, i ^ 1) for i in range(bl)])

    def fswap(value, bit):
        return lax.ppermute(value, "facet", [(i, i ^ bit) for i in range(nf)])

    def yshift(value, by):
        return lax.ppermute(value, "facet", [(i, (i + by * nf // 4) % nf) for i in range(nf)])

    place = jnp.stack([here, facet % 2]).astype(jnp.int32)

    block = pack(
        pltpu.with_memory_space_constraint(facet_model, pltpu.HBM),
        pltpu.with_memory_space_constraint(screens, pltpu.HBM),
    )
    up1, down1 = zshift(block, 1), zshift(block, -1)
    both = jnp.concatenate([offsets, stations], axis=0)
    both_far = swap(both)
    offs = jnp.concatenate([both[:tiles], both_far[:tiles]], axis=0)

    spot = jnp.arange(cells // NX, dtype=jnp.int32)
    pixel_u = fx + ((z + spot // rows) % nz * NX + xl) * rows + spot % rows
    pixel_v = fy + jnp.arange(cells, dtype=jnp.int32)
    cell = jnp.arange(width, dtype=jnp.int32)
    eu_c, eu_s = wave(cell, pixel_u, grid)
    ou_c, ou_s = wave(offs[:, 0], pixel_u, grid)
    ev_c, ev_s = wave(cell, pixel_v, grid)
    ov_c, ov_s = wave(offs[:, 1], pixel_v, grid)
    eu_1 = jnp.concatenate([eu_c, -eu_s], axis=0)
    eu_2 = jnp.concatenate([-eu_s, -eu_c], axis=0)
    ev_1 = jnp.concatenate([ev_c, ev_s], axis=0)
    ev_2 = jnp.concatenate([-ev_s, ev_c], axis=0)
    tab_u = (ou_c[:, None] * eu_1[None] + ou_s[:, None] * eu_2[None]).astype(narrow)
    tab_v = (ov_c[:, None] * ev_1[None] + ov_s[:, None] * ev_2[None]).astype(narrow)

    up2, down2 = zshift(up1, 1), zshift(down1, -1)
    up3, down3 = zshift(up2, 1), zshift(down2, -1)
    half = block.shape[0] // 2
    first, second = zshift(up3[:half], 1), zshift(down3[half:], -1)

    relative = [block, down1, down2, down3, first, up3, up2, up1]
    other = swap(predict_call("predict_far", tab_u, tab_v, relative, narrow, tiles, tiles, 4))

    gains = relative[: nz // 2 + 1] + [second] + relative[nz // 2 + 1 :]
    slim = [(tiles, narrow), (nz * own, narrow)]
    x, pool = gain_call(far_gain_kernel, "gain_far", own, nz, place, both_far, gains, slim)
    x = swap(x)
    s = predict_call("predict_own", tab_u, tab_v, relative, jnp.float32, 0, tiles, 4)
    part = tiles // 2
    wides = [(count, jnp.float32) for count in (tiles, part, part)]
    gain, keep, give = gain_call(
        own_gain_kernel, "gain_own", own, nz, place, both, [pool, x, s, other], wides
    )

    keep = keep + fswap(give, 1)
    sent = keep.astype(narrow)
    keep = sent.astype(jnp.float32) + fswap(sent, 2).astype(jnp.float32)
    sent = keep.astype(narrow)
    before, beyond, behind = yshift(sent, 1), yshift(sent, 2), yshift(sent, 3)
    keep = (sent.astype(jnp.float32) + beyond.astype(jnp.float32)) + (
        before.astype(jnp.float32) + behind.astype(jnp.float32)
    )
    others = fswap(keep, 1)
    residual, w = pl.pallas_call(
        residual_kernel,
        out_shape=[
            jax.ShapeDtypeStruct(observed.shape, jnp.float32),
            jax.ShapeDtypeStruct(observed.shape, narrow),
        ],
        in_specs=[pl.BlockSpec(memory_space=pltpu.SMEM)] * 2
        + [pl.BlockSpec(memory_space=pltpu.VMEM)] * 4,
        out_specs=[pl.BlockSpec(memory_space=pltpu.VMEM)] * 2,
        compiler_params=room(8),
        name="residual",
    )(place, counts, keep, others, observed, gain)
    def grid_rows(w, tab_v):
        w_re, w_im = w[..., :width], w[..., width:]
        stacked = jnp.concatenate(
            [jnp.concatenate([w_re, -w_im], axis=2), jnp.concatenate([w_im, w_re], axis=2)], axis=1
        )
        return jnp.einsum(
            "tuk,tky->tuy", stacked, tab_v, preferred_element_type=jnp.float32
        ).astype(narrow)

    def image(at, q, low, high):
        return jnp.einsum(
            "tkx,tky->xy",
            tab_u[at : at + tiles, :, low * rows : high * rows],
            q,
            preferred_element_type=jnp.float32,
        )

    def after(value, other):
        return value + jnp.minimum(jnp.abs(other[0, 0]), 0.0).astype(value.dtype)

    w_far = swap(w)
    q_own = grid_rows(w, tab_v[:tiles])
    spans = ((2, 7), (7, 8), (0, 2))
    owns = [image(0, q_own, *span) for span in spans]
    q_far = grid_rows(after(w_far, owns[0]), tab_v[tiles:])
    outer = (owns[0] + image(tiles, q_far, *spans[0])).reshape(5, rows, cells)

    cut = rows // 2
    opposite = outer[2].astype(narrow)
    a, b = zshift(opposite[:cut], 1), zshift(opposite[cut:], -1)
    q_late = after(q_far, a)
    inner = [mine + image(tiles, q_late, *span) for mine, span in zip(owns[1:], spans[1:])]
    inner = jnp.concatenate(inner, axis=0).reshape(3, rows, cells)
    up, down = fold(a, b, outer[1], outer[3], 0, cut)
    for add_up, add_down in ((outer[0], outer[4]), (inner[2], inner[0])):
        up, down = fold(zshift(up, 1), zshift(down, -1), add_up, add_down)
    up, down = zshift(up, 1), zshift(down, -1)
    scale = 1.0 / (32.0 * width * math.sqrt(tiles * bl))
    own_rows = inner[1] + up.astype(jnp.float32) + down.astype(jnp.float32)
    return (residual, (own_rows * scale)[None])


def solution(mesh):
    in_specs = (
        P("facet", "bl", None),
        P("facet", "bl", None, None),
        P("bl", None, None),
        P("bl", None),
        P("bl", None),
        P("bl"),
    )
    out_specs = (P("bl", None, None), P("facet", "bl", None))
    return jax.shard_map(
        per_device, mesh=mesh, in_specs=in_specs, out_specs=out_specs, check_vma=False
    )
```
